32 devices in a mesh: grp: 4 (over z), cp: 8 (over y, x, core).
Axes of the slice: x: 2, y: 2, z: 4, core: 2. Of those that a mesh axis runs over, the one named last changes fastest.
Arguments:
- query: bfloat16 [8192, 2048], P(('grp', 'cp')), may hold values from -6 to 6
- key: bfloat16 [8192, 512], P(('grp', 'cp')), may hold values from -6 to 6
- value: bfloat16 [8192, 512], P(('grp', 'cp')), may hold values from -6 to 6
- output_gradient: bfloat16 [8192, 2048], P(('grp', 'cp')), may hold values from -0.59765625 to 0.59765625
- lse: bfloat16 [8192, 16], P(('grp', 'cp')), may hold values from 1 to 3
- delta: bfloat16 [8192, 16], P(('grp', 'cp')), may hold values from -6 to 6
- lengths: int32 [4], replicated, may hold values from 1 to 4096, as said below
- plan: int32 [512], P(('grp', 'cp')), may hold values from -1 to 6, as said below
Outputs:
- dquery: bfloat16 [8192, 2048], P(('grp', 'cp'))
- dkey: bfloat16 [8192, 512], P(('grp', 'cp'))
- dvalue: bfloat16 [8192, 512], P(('grp', 'cp'))
The draws below stay inside these ranges and needn't reach their ends.
Inputs may be any that keep to these rules, and one draw needn't show every extreme that they name: `lengths`: in order; they sum to 8192, and the longest is 4096. `plan`: a block's entry is -1 or a member index of its own group below the member that holds the block, whose shard holds tokens of the document of the block's first row; the blocks of one device name distinct members.
All inputs are finite; a program needn't handle non-finite values.
Results may differ from the reference program's by a relative error of at most 0.0061.
Values may be sent and summed in bfloat16 or wider, within the bound.
A program may use at most 128 MiB of HBM per device.

```python
import jax
import jax.numpy as jnp
from jax import lax

QUERY_HEADS = 16
KEY_VALUE_HEADS = 4
HEAD_SIZE = 128
QB = 16
TOK_DEV = 256
ROUTED_BLOCKS = 16
PACKED_TOKENS = 8192
NBLOCKS = 512
NDOCS = 4
MOST_DOC = 4096
N_CP = 8
DEVICES = 32


def shared_lengths(key):
    base_key = jax.random.fold_in(key, 7717)
    count = NDOCS - 1
    rest = PACKED_TOKENS - MOST_DOC
    share = rest // count
    extra = rest - share * count
    others = (share + (jnp.arange(count, dtype=jnp.int32) < extra).astype(jnp.int32)).astype(jnp.int32)

    def mover(turn, current):
        turn_key = jax.random.fold_in(base_key, turn + 11)
        pair = jax.random.randint(jax.random.fold_in(turn_key, 1), (2,), 0, count, dtype=jnp.int32)
        first = pair[0]
        second = pair[1]
        room = jnp.minimum(MOST_DOC - current[first], current[second] - 1)
        amount = jax.random.randint(jax.random.fold_in(turn_key, 2), (), 0, room + 1, dtype=jnp.int32)
        return current.at[first].add(amount).at[second].add(-amount)
    others = lax.fori_loop(0, 4 * count, mover, others)
    full = jnp.concatenate([jnp.full((1,), MOST_DOC, jnp.int32), others])
    return jax.random.permutation(jax.random.fold_in(base_key, 3), full).astype(jnp.int32)


def draw_lengths(key, part):
    return shared_lengths(key)


def draw_plan(key, part):
    lengths = shared_lengths(key)
    ends = jnp.cumsum(lengths).astype(jnp.int32)
    starts = (ends - lengths).astype(jnp.int32)
    block_first = jnp.arange(NBLOCKS, dtype=jnp.int32) * QB
    block_doc = jnp.sum((ends[None, :] <= block_first[:, None]).astype(jnp.int32), axis=1)
    doc_start = starts[block_doc].reshape(DEVICES, ROUTED_BLOCKS)
    devices = jnp.arange(DEVICES, dtype=jnp.int32)
    group_member = devices % N_CP
    group_first = devices - group_member
    peer_devices = jnp.arange(N_CP, dtype=jnp.int32)
    owner_end = (group_first[:, None] + peer_devices[None, :]) * TOK_DEV + TOK_DEV
    eligible = (peer_devices[None, None, :] <= group_member[:, None, None] - 1) & (owner_end[:, None, :] > doc_start[:, :, None])
    extra_scores = jnp.where(peer_devices[None, None, :] == group_member[:, None, None] - 1, (1 << 20) * N_CP, 0).astype(jnp.int32)
    score_matrix = jax.random.randint(jax.random.fold_in(key, 5), (DEVICES, ROUTED_BLOCKS, N_CP), 0, 1 << 20, dtype=jnp.int32) * N_CP + peer_devices[None, None, :] + extra_scores

    def assign(index, carry):
        used, chosen = carry
        open_peer = lax.dynamic_index_in_dim(eligible, index, 1, False) & jnp.logical_not(used)
        marked = jnp.where(open_peer, lax.dynamic_index_in_dim(score_matrix, index, 1, False), -1)
        best = jnp.argmax(marked, axis=1).astype(jnp.int32)
        found = jnp.max(marked, axis=1) >= 0
        owner = jnp.where(found, best, -1).astype(jnp.int32)
        used = used | (peer_devices[None, :] == best[:, None]) & found[:, None]
        chosen = lax.dynamic_update_slice_in_dim(chosen, owner[:, None], index, 1)
        return (used, chosen)
    start = (jnp.zeros((DEVICES, N_CP), bool), jnp.full((DEVICES, ROUTED_BLOCKS), -1, jnp.int32))
    used, chosen = lax.fori_loop(0, ROUTED_BLOCKS, assign, start)
    return chosen.reshape(NBLOCKS).astype(jnp.int32)


def shard_levels(key, shape, cuts, smallest, high):
    def one(dim, shards_of):
        steps = jax.random.uniform(jax.random.fold_in(jax.random.fold_in(key, 6), dim), (shards_of,), jnp.float32, smallest / len(cuts), high / len(cuts))
        return jnp.repeat(jnp.exp(steps), shape[dim] // shards_of).reshape((-1,) + (1,) * (len(shape) - dim - 1))

    loudness = one(*cuts[0])
    for cut in cuts[1:]:
        loudness = loudness * one(*cut)
    return loudness


def bell_draw(stream_key, extent, deviation, limit, shards=(), kind=jnp.bfloat16):
    array = deviation * jax.random.normal(stream_key, extent, jnp.float32)
    if shards:
        array = array * shard_levels(stream_key, extent, shards, -0.22, 0.18)
    return jnp.clip(array, -limit, limit).astype(kind)


def setup_inputs(seed: int = 0) -> dict:
    arg_keys = jax.random.split(jax.random.key(seed), 9)
    return {
        "query": bell_draw(arg_keys[0], (PACKED_TOKENS, QUERY_HEADS * HEAD_SIZE), 1.0, 6.0, ((0, 32),)),
        "key": bell_draw(arg_keys[1], (PACKED_TOKENS, KEY_VALUE_HEADS * HEAD_SIZE), 1.0, 6.0, ((0, 32),)),
        "value": bell_draw(arg_keys[2], (PACKED_TOKENS, KEY_VALUE_HEADS * HEAD_SIZE), 1.0, 6.0, ((0, 32),)),
        "output_gradient": bell_draw(arg_keys[3], (PACKED_TOKENS, QUERY_HEADS * HEAD_SIZE), 0.1, 0.59765625, ((0, 32),)),
        "lse": jnp.clip(1.0 + 2.0 * jax.random.uniform(arg_keys[4], (PACKED_TOKENS, QUERY_HEADS), jnp.float32) ** shard_levels(arg_keys[4], (PACKED_TOKENS, QUERY_HEADS), ((0, 32),), -0.2, 0.2), 1.0, 3.0).astype(jnp.bfloat16),
        "delta": bell_draw(arg_keys[5], (PACKED_TOKENS, QUERY_HEADS), 1.0, 6.0, ((0, 32),)),
        "lengths": draw_lengths(jax.random.fold_in(arg_keys[8], 71), 0),
        "plan": draw_plan(jax.random.fold_in(arg_keys[8], 71), 0),
    }


def doc_ids(position, doc_ends):
    return jnp.sum((doc_ends[None, :] <= position[:, None]).astype(jnp.int32), axis=1).astype(jnp.int32)


def lowered(values):
    return lax.optimization_barrier(values.astype(jnp.bfloat16)).astype(jnp.float32)


def head_grads(queries, grad_rows, lse_rows, delta_rows, keys_head, values_head, allowed):
    factor = HEAD_SIZE ** -0.5
    score_matrix = jnp.einsum("rgd,cd->rgc", queries, keys_head) * factor
    shifted = jnp.where(allowed[:, None, :], score_matrix - lse_rows[:, :, None], -jnp.inf)
    probs = jnp.exp(shifted)
    dprobs = jnp.einsum("rgd,cd->rgc", grad_rows, values_head)
    dscores = probs * (dprobs - delta_rows[:, :, None])
    probs_low = lowered(probs)
    dscores_low = lowered(dscores)
    value_gradient = jnp.einsum("rgc,rgd->cd", probs_low, grad_rows)
    key_gradient = jnp.einsum("rgc,rgd->cd", dscores_low, queries) * factor
    grad_query = jnp.einsum("rgc,cd->rgd", dscores_low, keys_head) * factor
    return grad_query, key_gradient, value_gradient


def attention_grads(query, output_gradient, lse, delta, key, value, allowed):
    query_count = query.shape[0]
    key_count = key.shape[0]
    query_group = QUERY_HEADS // KEY_VALUE_HEADS
    query_per_head = jnp.moveaxis(query.astype(jnp.float32).reshape(query_count, KEY_VALUE_HEADS, query_group, HEAD_SIZE), 1, 0)
    gradient_per_head = jnp.moveaxis(output_gradient.astype(jnp.float32).reshape(query_count, KEY_VALUE_HEADS, query_group, HEAD_SIZE), 1, 0)
    logsumexp_per_head = jnp.moveaxis(lse.astype(jnp.float32).reshape(query_count, KEY_VALUE_HEADS, query_group), 1, 0)
    delta_per_head = jnp.moveaxis(delta.astype(jnp.float32).reshape(query_count, KEY_VALUE_HEADS, query_group), 1, 0)
    key_per_head = jnp.moveaxis(key.astype(jnp.float32).reshape(key_count, KEY_VALUE_HEADS, HEAD_SIZE), 1, 0)
    value_per_head = jnp.moveaxis(value.astype(jnp.float32).reshape(key_count, KEY_VALUE_HEADS, HEAD_SIZE), 1, 0)

    def per_head(pieces):
        return head_grads(pieces[0], pieces[1], pieces[2], pieces[3], pieces[4], pieces[5], allowed)

    grad_query, key_gradient, value_gradient = lax.map(per_head, (query_per_head, gradient_per_head, logsumexp_per_head, delta_per_head, key_per_head, value_per_head))
    return (jnp.moveaxis(grad_query, 0, 1).reshape(query_count, QUERY_HEADS * HEAD_SIZE),
            jnp.moveaxis(key_gradient, 0, 1).reshape(key_count, KEY_VALUE_HEADS * HEAD_SIZE),
            jnp.moveaxis(value_gradient, 0, 1).reshape(key_count, KEY_VALUE_HEADS * HEAD_SIZE))


def reference(query, key, value, output_gradient, lse, delta, lengths, plan):
    shard_count = PACKED_TOKENS // TOK_DEV
    block_count = TOK_DEV // QB
    key_value_width = KEY_VALUE_HEADS * HEAD_SIZE
    width_q = QUERY_HEADS * HEAD_SIZE
    doc_ends = jnp.cumsum(lengths).astype(jnp.int32)
    pad_rows = jnp.zeros((TOK_DEV, key_value_width), key.dtype)
    key_pad = jnp.concatenate([pad_rows, key], axis=0)
    value_pad = jnp.concatenate([pad_rows, value], axis=0)
    key_shards = key.reshape(shard_count, TOK_DEV, key_value_width)
    value_shards = value.reshape(shard_count, TOK_DEV, key_value_width)
    offsets = jnp.arange(TOK_DEV, dtype=jnp.int32)

    def step(carry, shard_id):
        dk_acc, dv_acc = carry
        first_row = shard_id * TOK_DEV
        rows_query = lax.dynamic_slice_in_dim(query, first_row, TOK_DEV, 0)
        rows_grad = lax.dynamic_slice_in_dim(output_gradient, first_row, TOK_DEV, 0)
        rows_lse = lax.dynamic_slice_in_dim(lse, first_row, TOK_DEV, 0)
        rows_delta = lax.dynamic_slice_in_dim(delta, first_row, TOK_DEV, 0)
        position = first_row + offsets
        own_doc = doc_ids(position, doc_ends)
        owners = lax.dynamic_slice_in_dim(plan, shard_id * block_count, block_count, 0)
        member_id = (shard_id % N_CP).astype(jnp.int32)
        owners_row = jnp.repeat(owners, QB)
        skip_prev = (owners_row == member_id - 1) & (member_id >= 1)
        key_rows = lax.dynamic_slice_in_dim(key_pad, first_row, 2 * TOK_DEV, 0)
        value_rows = lax.dynamic_slice_in_dim(value_pad, first_row, 2 * TOK_DEV, 0)
        key_pos = first_row - TOK_DEV + jnp.arange(2 * TOK_DEV, dtype=jnp.int32)
        key_doc = doc_ids(key_pos, doc_ends)
        allowed = (own_doc[:, None] == key_doc[None, :]) & (key_pos[None, :] <= position[:, None]) & (key_pos[None, :] >= 0)
        allowed = allowed & jnp.logical_not(skip_prev[:, None] & (key_pos[None, :] < first_row))
        dq_local, dk_local, dv_local = attention_grads(rows_query, rows_grad, rows_lse, rows_delta, key_rows, value_rows, allowed)
        dk_acc = lax.dynamic_update_slice_in_dim(dk_acc, lax.dynamic_slice_in_dim(dk_acc, shard_id, 2, 0) + dk_local.reshape(2, TOK_DEV, key_value_width), shard_id, 0)
        dv_acc = lax.dynamic_update_slice_in_dim(dv_acc, lax.dynamic_slice_in_dim(dv_acc, shard_id, 2, 0) + dv_local.reshape(2, TOK_DEV, key_value_width), shard_id, 0)
        group_first = (shard_id // N_CP) * N_CP
        owner_shard = (group_first + jnp.maximum(owners, 0)).astype(jnp.int32)
        live_block = owners >= 0
        block_key = key_shards[owner_shard]
        block_value = value_shards[owner_shard]
        block_key_pos = owner_shard[:, None] * TOK_DEV + offsets[None, :]
        block_pos = position.reshape(block_count, QB)

        def one_block(b_query, b_grad, b_lse, b_delta, b_key, b_value, b_pos, b_key_pos, b_live):
            allowed_block = b_live & (doc_ids(b_pos, doc_ends)[:, None] == doc_ids(b_key_pos, doc_ends)[None, :]) & (b_key_pos[None, :] <= b_pos[:, None])
            return attention_grads(b_query, b_grad, b_lse, b_delta, b_key, b_value, allowed_block)

        dq_block, dk_block, dv_block = jax.vmap(one_block)(
            rows_query.reshape(block_count, QB, width_q), rows_grad.reshape(block_count, QB, width_q),
            rows_lse.reshape(block_count, QB, QUERY_HEADS), rows_delta.reshape(block_count, QB, QUERY_HEADS),
            block_key, block_value, block_pos, block_key_pos, live_block)
        dk_acc = dk_acc.at[owner_shard + 1].add(dk_block)
        dv_acc = dv_acc.at[owner_shard + 1].add(dv_block)
        grad_query = (dq_local + dq_block.reshape(TOK_DEV, width_q)).astype(jnp.bfloat16)
        return (dk_acc, dv_acc), grad_query

    zeros = jnp.zeros((shard_count + 1, TOK_DEV, key_value_width), jnp.float32)
    (dk_acc, dv_acc), dquery = lax.scan(step, (zeros, zeros), jnp.arange(shard_count, dtype=jnp.int32))
    dkey = dk_acc[1:].reshape(PACKED_TOKENS, key_value_width).astype(jnp.bfloat16)
    dvalue = dv_acc[1:].reshape(PACKED_TOKENS, key_value_width).astype(jnp.bfloat16)
    return dquery.reshape(PACKED_TOKENS, width_q), dkey, dvalue
```

```python
import functools
import math

import jax
import jax.numpy as jnp
from jax import lax
from jax.experimental import pallas as pl
from jax.experimental.pallas import tpu as pltpu
from jax.sharding import PartitionSpec as P

HEAD_SIZE = 128
FACTOR = HEAD_SIZE**-0.5
LOG2E = math.log2(math.e)
F32 = jnp.float32
BF16 = jnp.bfloat16
MESH = pl.DeviceIdType.MESH


def dot_nt(a, b):
    return lax.dot_general(a, b, (((1,), (1,)), ((), ())), preferred_element_type=F32)


def dot_nn(a, b):
    return jnp.dot(a, b, preferred_element_type=F32)


def group_grads(queries, grads, lse_rows, delta_rows, keys, values, bias):
    keys_t = keys.T
    probs_low, dscores_low, grad_query = [], [], []
    for q, do, lse, delta in zip(queries, grads, lse_rows, delta_rows):
        scores = dot_nt(keys, q)
        probs = jnp.exp2(scores * (FACTOR * LOG2E) + (bias - lse))
        dscores = probs * (dot_nt(values, do) - delta)
        probs_low.append(probs.astype(BF16))
        dscores_low.append(dscores.astype(BF16))
        grad_query.append(dot_nn(keys_t, dscores_low[-1]))
    dv = dot_nn(jnp.concatenate(probs_low, axis=1), jnp.concatenate(grads, axis=0))
    dk = dot_nn(jnp.concatenate(dscores_low, axis=1), jnp.concatenate(queries, axis=0))
    return grad_query, dk, dv


def kernel(
    n,
    groups,
    lengths,
    plan,
    q_ref,
    do_ref,
    k_ref,
    v_ref,
    lse_ref,
    delta_ref,
    dq_ref,
    dk_ref,
    dv_ref,
    slot_out,
    slot_in,
    stat_out,
    stat_in,
    k_prev,
    v_prev,
    back_out,
    back_in,
    dq_out,
    dq_in,
    pick_t,
    stats_t,
    bias_own,
    bias_prev,
    bias_in,
    routed_t,
    dq_t,
    dq_acc,
    dk_acc,
    dv_acc,
    slot_send,
    slot_recv,
    stat_send,
    stat_recv,
    kv_send,
    kv_recv,
    back_send,
    back_recv,
    dqs_send,
    dqs_recv,
):
    grp = lax.axis_index("grp")
    me = lax.axis_index("cp")
    shard = grp * n + me
    last = groups * n - 1
    rows, width_q = q_ref.shape
    width_k = k_ref.shape[1]
    heads = width_q // HEAD_SIZE
    kv_heads = width_k // HEAD_SIZE
    per = heads // kv_heads
    blocks = plan.shape[0]
    block = rows // blocks
    ndocs = lengths.shape[0]
    base = shard * rows
    right = (jnp.where(me == n - 1, jnp.minimum(grp + 1, groups - 1), grp), lax.rem(me + 1, n))
    left = (jnp.where(me == 0, jnp.maximum(grp - 1, 0), grp), lax.rem(me + n - 1, n))
    cross_right = (me == n - 1) & (grp < groups - 1)
    cross_left = (me == 0) & (grp > 0)
    sends = jnp.maximum(me - 1, 0)

    barrier = pltpu.get_barrier_semaphore()

    def greet(step, carry):
        peer = lax.rem(me + step, n)
        pl.semaphore_signal(barrier, inc=1, device_id=(grp, peer), device_id_type=MESH)
        return carry

    lax.fori_loop(1, n, greet, 0)

    @pl.when(cross_right)
    def _():
        pl.semaphore_signal(barrier, inc=1, device_id=right, device_id_type=MESH)

    @pl.when(cross_left)
    def _():
        pl.semaphore_signal(barrier, inc=1, device_id=left, device_id_type=MESH)

    pos = base + lax.broadcasted_iota(jnp.int32, (8, rows), 1)
    start = jnp.zeros((8, rows), jnp.int32)
    end = jnp.int32(0)
    for d in range(ndocs):
        end = end + lengths[d]
        start = jnp.where(pos >= end, end, start)
    lse_rows = lse_ref[...].astype(F32) * LOG2E
    delta_rows = delta_ref[...].astype(F32)
    pad = HEAD_SIZE - 2 * heads - 16
    packed = jnp.concatenate(
        [
            lse_rows,
            delta_rows,
            start.astype(F32),
            jnp.ones((8, rows), F32),
            jnp.zeros((pad, rows), F32),
        ],
        axis=0,
    )
    stats_t[...] = packed

    count = n * block
    owner = jnp.full((8, rows), -1, jnp.int32)
    token = lax.broadcasted_iota(jnp.int32, (8, rows), 1)
    for b in range(blocks):
        owner = jnp.where((token >= b * block) & (token < (b + 1) * block), plan[b], owner)
    within = lax.rem(token, block)
    slot_row = lax.broadcasted_iota(jnp.int32, (count, rows), 0)
    wanted = owner[:1] * block + within[:1]
    pick = jnp.where((slot_row == wanted) & (owner[:1] >= 0), 1.0, 0.0)
    pick_low = pick.astype(BF16)
    pick_t[...] = pick.T.astype(BF16)
    slot_out[:, :, :width_q] = dot_nn(pick_low, q_ref[...]).astype(BF16).reshape(n, block, width_q)
    slot_out[:, :, width_q:] = dot_nn(pick_low, do_ref[...]).astype(BF16).reshape(n, block, width_q)
    stat_out[...] = jnp.dot(
        pick, packed.T, preferred_element_type=F32, precision=lax.Precision.HIGHEST
    ).reshape(n, block, HEAD_SIZE)

    def blank_in(p, carry):
        slot_in[p] = jnp.zeros(slot_in.shape[1:], BF16)
        stat_in[p] = jnp.zeros(stat_in.shape[1:], F32)
        return carry

    lax.fori_loop(0, jnp.minimum(me + 2, n), blank_in, 0)

    def blank_dq(p, carry):
        dq_in[p] = jnp.zeros(dq_in.shape[1:], BF16)
        return carry

    lax.fori_loop(sends, n, blank_dq, 0)

    @pl.when(shard == 0)
    def _():
        k_prev[...] = jnp.zeros_like(k_prev)
        v_prev[...] = jnp.zeros_like(v_prev)

    @pl.when(shard == last)
    def _():
        back_in[...] = jnp.zeros_like(back_in)

    pl.semaphore_wait(barrier, n - 1 + cross_right.astype(jnp.int32) + cross_left.astype(jnp.int32))

    def kv_copies():
        return (
            pltpu.make_async_remote_copy(
                k_ref, k_prev, kv_send.at[0], kv_recv.at[0], device_id=right, device_id_type=MESH
            ),
            pltpu.make_async_remote_copy(
                v_ref, v_prev, kv_send.at[1], kv_recv.at[1], device_id=right, device_id_type=MESH
            ),
        )

    def slot_copies(p, src):
        return (
            pltpu.make_async_remote_copy(
                slot_out.at[p],
                slot_in.at[src],
                slot_send.at[p],
                slot_recv.at[src],
                device_id=(grp, p),
                device_id_type=MESH,
            ),
            pltpu.make_async_remote_copy(
                stat_out.at[p],
                stat_in.at[src],
                stat_send.at[p],
                stat_recv.at[src],
                device_id=(grp, p),
                device_id_type=MESH,
            ),
        )

    def dq_copy(m, src):
        return pltpu.make_async_remote_copy(
            dq_out.at[m],
            dq_in.at[src],
            dqs_send.at[m],
            dqs_recv.at[src],
            device_id=(grp, m),
            device_id_type=MESH,
        )

    def back_copy(g):
        return pltpu.make_async_remote_copy(
            back_out.at[g],
            back_in.at[g],
            back_send.at[g],
            back_recv.at[g],
            device_id=left,
            device_id_type=MESH,
        )

    @pl.when(shard < last)
    def _():
        for copy in kv_copies():
            copy.start()

    def send(p, carry):
        for copy in slot_copies(p, me):
            copy.start()
        return carry

    lax.fori_loop(0, sends, send, 0)

    key_at = lax.broadcasted_iota(jnp.int32, (rows, rows), 0)
    query_at = lax.broadcasted_iota(jnp.int32, (rows, rows), 1)
    begin = start[:1] - base
    bias_own[...] = jnp.where((key_at <= query_at) & (key_at >= begin), 0.0, -jnp.inf)
    bias_prev[...] = jnp.where(key_at - rows >= begin, 0.0, -jnp.inf)

    def columns(h):
        return pl.ds(pl.multiple_of(h * HEAD_SIZE, HEAD_SIZE), HEAD_SIZE)

    def local_inputs(g):
        hs = [g * per + u for u in range(per)]
        return (
            [q_ref[:, columns(h)] for h in hs],
            [do_ref[:, columns(h)] for h in hs],
            [stats_t[pl.ds(h, 1), :] for h in hs],
            [stats_t[pl.ds(heads + h, 1), :] for h in hs],
        )

    def own(g, carry):
        cols = columns(g)
        grad_query, dk, dv = group_grads(
            *local_inputs(g), k_ref[:, cols], v_ref[:, cols], bias_own[...]
        )
        for u in range(per):
            dq_t[columns(g * per + u), :] = grad_query[u]
        dk_acc[:, cols] = dk
        dv_acc[:, cols] = dv
        return carry

    lax.fori_loop(0, kv_heads, own, 0)

    @pl.when(shard > 0)
    def _():
        for copy in kv_copies():
            copy.wait_recv()

    def prev(g, carry):
        cols = columns(g)
        grad_query, dk, dv = group_grads(
            *local_inputs(g), k_prev[:, cols], v_prev[:, cols], bias_prev[...]
        )
        for u in range(per):
            where = columns(g * per + u)
            dq_acc[:, where] = ((dq_t[where, :] + grad_query[u]) * FACTOR).T
        back_out[g, 0] = (dk * FACTOR).astype(BF16)
        back_out[g, 1] = dv.astype(BF16)

        @pl.when(shard > 0)
        def _():
            back_copy(g).start()

        return carry

    lax.fori_loop(0, kv_heads, prev, 0)

    def arrive(m, carry):
        for copy in slot_copies(m, m):
            copy.wait_recv()
        return carry

    lax.fori_loop(me + 2, n, arrive, 0)

    @pl.when(me + 2 < n)
    def _():
        routed_t[...] = stat_in[...].reshape(count, HEAD_SIZE).T
        key_pos = base + lax.broadcasted_iota(jnp.int32, (rows, count), 0)
        first = routed_t[pl.ds(2 * heads, 1), :]
        live = routed_t[pl.ds(2 * heads + 8, 1), :] > 0.5
        bias_in[...] = jnp.where((key_pos.astype(F32) >= first) & live, 0.0, -jnp.inf)

        def routed(g, carry):
            cols = columns(g)
            hs = [g * per + u for u in range(per)]
            grad_query, dk, dv = group_grads(
                [slot_in[:, :, columns(h)].reshape(count, HEAD_SIZE) for h in hs],
                [slot_in[:, :, columns(heads + h)].reshape(count, HEAD_SIZE) for h in hs],
                [routed_t[pl.ds(h, 1), :] for h in hs],
                [routed_t[pl.ds(heads + h, 1), :] for h in hs],
                k_ref[:, cols],
                v_ref[:, cols],
                bias_in[...],
            )
            for u in range(per):
                dq_out[:, :, columns(hs[u])] = (
                    (grad_query[u] * FACTOR).T.astype(BF16).reshape(n, block, HEAD_SIZE)
                )
            dk_acc[:, cols] += dk
            dv_acc[:, cols] += dv
            return carry

        lax.fori_loop(0, kv_heads, routed, 0)

        def give_back(m, carry):
            dq_copy(m, me).start()
            return carry

        lax.fori_loop(me + 2, n, give_back, 0)

    for g in range(kv_heads):

        @pl.when(shard < last)
        def _(g=g):
            back_copy(g).wait_recv()

        cols = pl.ds(g * HEAD_SIZE, HEAD_SIZE)
        dk_ref[:, cols] = (dk_acc[:, cols] * FACTOR + back_in[g, 0].astype(F32)).astype(BF16)
        dv_ref[:, cols] = (dv_acc[:, cols] + back_in[g, 1].astype(F32)).astype(BF16)

    def take(p, carry):
        dq_copy(p, p).wait_recv()
        return carry

    lax.fori_loop(0, sends, take, 0)

    def finish(h, carry):
        cols = columns(h)
        extra = dot_nn(pick_t[...], dq_in[:, :, cols].reshape(count, HEAD_SIZE))
        dq_ref[:, cols] = (dq_acc[:, cols] + extra).astype(BF16)
        return carry

    lax.fori_loop(0, heads, finish, 0)

    @pl.when(shard < last)
    def _():
        for copy in kv_copies():
            copy.wait_send()

    @pl.when(shard > 0)
    def _():
        for g in range(kv_heads):
            back_copy(g).wait_send()

    def sent(p, carry):
        for copy in slot_copies(p, me):
            copy.wait_send()
        return carry

    lax.fori_loop(0, sends, sent, 0)

    def sent_back(m, carry):
        dq_copy(m, me).wait_send()
        return carry

    lax.fori_loop(me + 2, n, sent_back, 0)


def on_device(query, key, value, output_gradient, lse, delta, lengths, plan):
    n = lax.axis_size("cp")
    groups = lax.axis_size("grp")
    rows, width_q = query.shape
    width_k = key.shape[1]
    kv_heads = width_k // HEAD_SIZE
    block = rows // plan.shape[0]
    vmem = pl.BlockSpec(memory_space=pltpu.VMEM)
    smem = pl.BlockSpec(memory_space=pltpu.SMEM)
    dma = pltpu.SemaphoreType.DMA
    return pl.pallas_call(
        functools.partial(kernel, n, groups),
        out_shape=(
            jax.ShapeDtypeStruct((rows, width_q), BF16),
            jax.ShapeDtypeStruct((rows, width_k), BF16),
            jax.ShapeDtypeStruct((rows, width_k), BF16),
        ),
        in_specs=[smem, smem] + [vmem] * 6,
        out_specs=[vmem] * 3,
        scratch_shapes=[
            pltpu.VMEM((n, block, 2 * width_q), BF16),
            pltpu.VMEM((n, block, 2 * width_q), BF16),
            pltpu.VMEM((n, block, HEAD_SIZE), F32),
            pltpu.VMEM((n, block, HEAD_SIZE), F32),
            pltpu.VMEM((rows, width_k), BF16),
            pltpu.VMEM((rows, width_k), BF16),
            pltpu.VMEM((kv_heads, 2, rows, HEAD_SIZE), BF16),
            pltpu.VMEM((kv_heads, 2, rows, HEAD_SIZE), BF16),
            pltpu.VMEM((n, block, width_q), BF16),
            pltpu.VMEM((n, block, width_q), BF16),
            pltpu.VMEM((rows, n * block), BF16),
            pltpu.VMEM((HEAD_SIZE, rows), F32),
            pltpu.VMEM((rows, rows), F32),
            pltpu.VMEM((rows, rows), F32),
            pltpu.VMEM((rows, n * block), F32),
            pltpu.VMEM((HEAD_SIZE, n * block), F32),
            pltpu.VMEM((width_q, rows), F32),
            pltpu.VMEM((rows, width_q), F32),
            pltpu.VMEM((rows, width_k), F32),
            pltpu.VMEM((rows, width_k), F32),
            dma((n,)),
            dma((n,)),
            dma((n,)),
            dma((n,)),
            dma((2,)),
            dma((2,)),
            dma((kv_heads,)),
            dma((kv_heads,)),
            dma((n,)),
            dma((n,)),
        ],
        compiler_params=pltpu.CompilerParams(
            collective_id=0, has_side_effects=True, vmem_limit_bytes=56 * 1024 * 1024
        ),
    )(lengths, plan, query, output_gradient, key, value, lse.T, delta.T)


def solution(mesh):
    rows = P(("grp", "cp"), None)
    return jax.shard_map(
        on_device,
        mesh=mesh,
        in_specs=(rows,) * 6 + (P(), P(("grp", "cp"))),
        out_specs=(rows,) * 3,
        check_vma=False,
    )
```

```python
import functools
import math

import jax
import jax.numpy as jnp
from jax import lax
from jax.experimental import pallas as pl
from jax.experimental.pallas import tpu as pltpu
from jax.sharding import PartitionSpec as P

HEAD_SIZE = 128
FACTOR = HEAD_SIZE**-0.5
LOG2E = math.log2(math.e)
F32 = jnp.float32
BF16 = jnp.bfloat16
MESH = pl.DeviceIdType.MESH


def dot_nt(a, b):
    return lax.dot_general(a, b, (((1,), (1,)), ((), ())), preferred_element_type=F32)


def dot_nn(a, b):
    return jnp.dot(a, b, preferred_element_type=F32)


def group_grads(queries, grads, lse_rows, delta_rows, keys, values, bias):
    keys_t = keys.T
    probs_low, dscores_low, grad_query = [], [], []
    for q, do, lse, delta in zip(queries, grads, lse_rows, delta_rows):
        scores = dot_nt(keys, q)
        probs = jnp.exp2(scores * (FACTOR * LOG2E) + (bias - lse))
        dscores = probs * (dot_nt(values, do) - delta)
        probs_low.append(probs.astype(BF16))
        dscores_low.append(dscores.astype(BF16))
        grad_query.append(dot_nn(keys_t, dscores_low[-1]))
    dv = dot_nn(jnp.concatenate(probs_low, axis=1), jnp.concatenate(grads, axis=0))
    dk = dot_nn(jnp.concatenate(dscores_low, axis=1), jnp.concatenate(queries, axis=0))
    return grad_query, dk, dv


def kernel(
    n,
    groups,
    lengths,
    plan,
    q_hbm,
    do_hbm,
    k_hbm,
    v_hbm,
    lse_ref,
    delta_ref,
    dq_ref,
    dk_ref,
    dv_ref,
    q_ref,
    do_ref,
    k_ref,
    v_ref,
    slot_out,
    slot_in,
    stat_out,
    stat_in,
    k_prev,
    v_prev,
    back_out,
    back_in,
    dq_out,
    dq_in,
    pick_t,
    stats_t,
    bias_own,
    bias_prev,
    bias_in,
    routed_t,
    dq_t,
    dq_acc,
    dk_acc,
    dv_acc,
    slot_send,
    slot_recv,
    stat_send,
    stat_recv,
    kv_send,
    kv_recv,
    back_send,
    back_recv,
    dqs_send,
    dqs_recv,
    load_sem,
):
    grp = lax.axis_index("grp")
    me = lax.axis_index("cp")
    shard = grp * n + me
    last = groups * n - 1
    rows, width_q = q_ref.shape
    width_k = k_ref.shape[1]
    heads = width_q // HEAD_SIZE
    kv_heads = width_k // HEAD_SIZE
    per = heads // kv_heads
    blocks = plan.shape[0]
    block = rows // blocks
    ndocs = lengths.shape[0]
    base = shard * rows
    right = (jnp.where(me == n - 1, jnp.minimum(grp + 1, groups - 1), grp), lax.rem(me + 1, n))
    left = (jnp.where(me == 0, jnp.maximum(grp - 1, 0), grp), lax.rem(me + n - 1, n))
    cross_right = (me == n - 1) & (grp < groups - 1)
    cross_left = (me == 0) & (grp > 0)
    sends = jnp.maximum(me - 1, 0)

    barrier = pltpu.get_barrier_semaphore()
    loads = [
        pltpu.make_async_copy(source, target, load_sem.at[i])
        for i, (source, target) in enumerate(
            ((q_hbm, q_ref), (do_hbm, do_ref), (k_hbm, k_ref), (v_hbm, v_ref))
        )
    ]
    for load in loads:
        load.start()

    def greet(step, carry):
        peer = lax.rem(me + step, n)
        pl.semaphore_signal(barrier, inc=1, device_id=(grp, peer), device_id_type=MESH)
        return carry

    lax.fori_loop(1, n, greet, 0)

    @pl.when(cross_right)
    def _():
        pl.semaphore_signal(barrier, inc=1, device_id=right, device_id_type=MESH)

    @pl.when(cross_left)
    def _():
        pl.semaphore_signal(barrier, inc=1, device_id=left, device_id_type=MESH)

    pos = base + lax.broadcasted_iota(jnp.int32, (8, rows), 1)
    start = jnp.zeros((8, rows), jnp.int32)
    end = jnp.int32(0)
    for d in range(ndocs):
        end = end + lengths[d]
        start = jnp.where(pos >= end, end, start)
    lse_rows = lse_ref[...].astype(F32) * LOG2E
    delta_rows = delta_ref[...].astype(F32)
    pad = HEAD_SIZE - 2 * heads - 16
    packed = jnp.concatenate(
        [
            lse_rows,
            delta_rows,
            start.astype(F32),
            jnp.ones((8, rows), F32),
            jnp.zeros((pad, rows), F32),
        ],
        axis=0,
    )
    stats_t[...] = packed

    count = n * block
    owner = jnp.full((8, rows), -1, jnp.int32)
    token = lax.broadcasted_iota(jnp.int32, (8, rows), 1)
    for b in range(blocks):
        owner = jnp.where((token >= b * block) & (token < (b + 1) * block), plan[b], owner)
    within = lax.rem(token, block)
    slot_row = lax.broadcasted_iota(jnp.int32, (count, rows), 0)
    wanted = owner[:1] * block + within[:1]
    pick = jnp.where((slot_row == wanted) & (owner[:1] >= 0), 1.0, 0.0)
    pick_low = pick.astype(BF16)
    pick_t[...] = pick.T.astype(BF16)
    loads[0].wait()
    slot_out[:, :, :width_q] = dot_nn(pick_low, q_ref[...]).astype(BF16).reshape(n, block, width_q)
    loads[1].wait()
    slot_out[:, :, width_q:] = dot_nn(pick_low, do_ref[...]).astype(BF16).reshape(n, block, width_q)
    stat_out[...] = jnp.dot(
        pick, packed.T, preferred_element_type=F32, precision=lax.Precision.HIGHEST
    ).reshape(n, block, HEAD_SIZE)

    def blank_in(p, carry):
        slot_in[p] = jnp.zeros(slot_in.shape[1:], BF16)
        stat_in[p] = jnp.zeros(stat_in.shape[1:], F32)
        return carry

    lax.fori_loop(0, jnp.minimum(me + 2, n), blank_in, 0)

    def blank_dq(p, carry):
        dq_in[p] = jnp.zeros(dq_in.shape[1:], BF16)
        return carry

    lax.fori_loop(sends, n, blank_dq, 0)

    @pl.when(shard == 0)
    def _():
        k_prev[...] = jnp.zeros_like(k_prev)
        v_prev[...] = jnp.zeros_like(v_prev)

    @pl.when(shard == last)
    def _():
        back_in[...] = jnp.zeros_like(back_in)

    pl.semaphore_wait(barrier, n - 1 + cross_right.astype(jnp.int32) + cross_left.astype(jnp.int32))

    def kv_copies():
        return (
            pltpu.make_async_remote_copy(
                k_hbm, k_prev, kv_send.at[0], kv_recv.at[0], device_id=right, device_id_type=MESH
            ),
            pltpu.make_async_remote_copy(
                v_hbm, v_prev, kv_send.at[1], kv_recv.at[1], device_id=right, device_id_type=MESH
            ),
        )

    def slot_copies(p, src):
        return (
            pltpu.make_async_remote_copy(
                slot_out.at[p],
                slot_in.at[src],
                slot_send.at[p],
                slot_recv.at[src],
                device_id=(grp, p),
                device_id_type=MESH,
            ),
            pltpu.make_async_remote_copy(
                stat_out.at[p],
                stat_in.at[src],
                stat_send.at[p],
                stat_recv.at[src],
                device_id=(grp, p),
                device_id_type=MESH,
            ),
        )

    def dq_copy(m, src):
        return pltpu.make_async_remote_copy(
            dq_out.at[m],
            dq_in.at[src],
            dqs_send.at[m],
            dqs_recv.at[src],
            device_id=(grp, m),
            device_id_type=MESH,
        )

    def back_copy(g):
        return pltpu.make_async_remote_copy(
            back_out.at[g],
            back_in.at[g],
            back_send.at[g],
            back_recv.at[g],
            device_id=left,
            device_id_type=MESH,
        )

    @pl.when(shard < last)
    def _():
        for copy in kv_copies():
            copy.start()

    def send(p, carry):
        for copy in slot_copies(p, me):
            copy.start()
        return carry

    lax.fori_loop(0, sends, send, 0)

    key_at = lax.broadcasted_iota(jnp.int32, (rows, rows), 0)
    query_at = lax.broadcasted_iota(jnp.int32, (rows, rows), 1)
    begin = start[:1] - base
    bias_own[...] = jnp.where((key_at <= query_at) & (key_at >= begin), 0.0, -jnp.inf)
    bias_prev[...] = jnp.where(key_at - rows >= begin, 0.0, -jnp.inf)

    def columns(h):
        return pl.ds(pl.multiple_of(h * HEAD_SIZE, HEAD_SIZE), HEAD_SIZE)

    def local_inputs(g):
        hs = [g * per + u for u in range(per)]
        return (
            [q_ref[:, columns(h)] for h in hs],
            [do_ref[:, columns(h)] for h in hs],
            [stats_t[pl.ds(h, 1), :] for h in hs],
            [stats_t[pl.ds(heads + h, 1), :] for h in hs],
        )

    def own(g, carry):
        cols = columns(g)
        grad_query, dk, dv = group_grads(
            *local_inputs(g), k_ref[:, cols], v_ref[:, cols], bias_own[...]
        )
        for u in range(per):
            dq_t[columns(g * per + u), :] = grad_query[u]
        dk_acc[:, cols] = dk
        dv_acc[:, cols] = dv
        return carry

    loads[2].wait()
    loads[3].wait()
    lax.fori_loop(0, kv_heads, own, 0)

    @pl.when(shard > 0)
    def _():
        for copy in kv_copies():
            copy.wait_recv()

    def prev(g, carry):
        cols = columns(g)
        grad_query, dk, dv = group_grads(
            *local_inputs(g), k_prev[:, cols], v_prev[:, cols], bias_prev[...]
        )
        for u in range(per):
            where = columns(g * per + u)
            dq_acc[:, where] = ((dq_t[where, :] + grad_query[u]) * FACTOR).T
        back_out[g, 0] = (dk * FACTOR).astype(BF16)
        back_out[g, 1] = dv.astype(BF16)

        @pl.when(shard > 0)
        def _():
            back_copy(g).start()

        return carry

    lax.fori_loop(0, kv_heads, prev, 0)

    half = 2 * block
    lanes = per * half
    lane_head = lax.broadcasted_iota(jnp.int32, (1, lanes), 1) // half
    key_pos = base + lax.broadcasted_iota(jnp.int32, (rows, lanes), 0)

    def batch(j, carry):
        m = 2 * j

        @pl.when(m >= me + 2)
        def _():
            for copy in slot_copies(m, m):
                copy.wait_recv()

        for copy in slot_copies(m + 1, m + 1):
            copy.wait_recv()
        pair = pl.ds(m, 2)
        stat = stat_in[pair].reshape(half, HEAD_SIZE)
        routed_t[...] = jnp.concatenate([stat] * per, axis=0).T
        first = routed_t[pl.ds(2 * heads, 1), :]
        live = routed_t[pl.ds(2 * heads + 8, 1), :] > 0.5
        bias_in[...] = jnp.where((key_pos.astype(F32) >= first) & live, 0.0, -jnp.inf)

        def row_of(first_row):
            out = routed_t[pl.ds(first_row, 1), :]
            for u in range(1, per):
                out = jnp.where(lane_head == u, routed_t[pl.ds(first_row + u, 1), :], out)
            return out

        def routed(g, carry):
            cols = columns(g)
            hs = [g * per + u for u in range(per)]

            def stack(offset):
                return jnp.concatenate(
                    [
                        slot_in[pair, :, columns(offset + h)].reshape(half, HEAD_SIZE)
                        for h in hs
                    ],
                    axis=0,
                )

            grad_query, dk, dv = group_grads(
                [stack(0)],
                [stack(heads)],
                [row_of(g * per)],
                [row_of(heads + g * per)],
                k_ref[:, cols],
                v_ref[:, cols],
                bias_in[...],
            )
            back = (grad_query[0] * FACTOR).T.astype(BF16)
            for u in range(per):
                dq_out[pair, :, columns(hs[u])] = back[u * half : (u + 1) * half].reshape(
                    2, block, HEAD_SIZE
                )
            dk_acc[:, cols] += dk
            dv_acc[:, cols] += dv
            return carry

        lax.fori_loop(0, kv_heads, routed, 0)

        @pl.when(m >= me + 2)
        def _():
            dq_copy(m, me).start()

        dq_copy(m + 1, me).start()
        return carry

    lax.fori_loop((me + 2) // 2, n // 2, batch, 0)

    for g in range(kv_heads):

        @pl.when(shard < last)
        def _(g=g):
            back_copy(g).wait_recv()

        cols = pl.ds(g * HEAD_SIZE, HEAD_SIZE)
        dk_ref[:, cols] = (dk_acc[:, cols] * FACTOR + back_in[g, 0].astype(F32)).astype(BF16)
        dv_ref[:, cols] = (dv_acc[:, cols] + back_in[g, 1].astype(F32)).astype(BF16)

    def take(p, carry):
        dq_copy(p, p).wait_recv()
        return carry

    lax.fori_loop(0, sends, take, 0)

    def finish(h, carry):
        cols = columns(h)
        extra = dot_nn(pick_t[...], dq_in[:, :, cols].reshape(count, HEAD_SIZE))
        dq_ref[:, cols] = (dq_acc[:, cols] + extra).astype(BF16)
        return carry

    lax.fori_loop(0, heads, finish, 0)

    @pl.when(shard < last)
    def _():
        for copy in kv_copies():
            copy.wait_send()

    @pl.when(shard > 0)
    def _():
        for g in range(kv_heads):
            back_copy(g).wait_send()

    def sent(p, carry):
        for copy in slot_copies(p, me):
            copy.wait_send()
        return carry

    lax.fori_loop(0, sends, sent, 0)

    def sent_back(m, carry):
        dq_copy(m, me).wait_send()
        return carry

    lax.fori_loop(me + 2, n, sent_back, 0)


def on_device(query, key, value, output_gradient, lse, delta, lengths, plan):
    n = lax.axis_size("cp")
    groups = lax.axis_size("grp")
    rows, width_q = query.shape
    width_k = key.shape[1]
    kv_heads = width_k // HEAD_SIZE
    block = rows // plan.shape[0]
    lanes = 2 * block * (width_q // width_k)
    vmem = pl.BlockSpec(memory_space=pltpu.VMEM)
    smem = pl.BlockSpec(memory_space=pltpu.SMEM)
    dma = pltpu.SemaphoreType.DMA
    return pl.pallas_call(
        functools.partial(kernel, n, groups),
        out_shape=(
            jax.ShapeDtypeStruct((rows, width_q), BF16),
            jax.ShapeDtypeStruct((rows, width_k), BF16),
            jax.ShapeDtypeStruct((rows, width_k), BF16),
        ),
        in_specs=[smem, smem] + [pl.BlockSpec(memory_space=pl.ANY)] * 4 + [vmem] * 2,
        out_specs=[vmem] * 3,
        scratch_shapes=[
            pltpu.VMEM((rows, width_q), BF16),
            pltpu.VMEM((rows, width_q), BF16),
            pltpu.VMEM((rows, width_k), BF16),
            pltpu.VMEM((rows, width_k), BF16),
            pltpu.VMEM((n, block, 2 * width_q), BF16),
            pltpu.VMEM((n, block, 2 * width_q), BF16),
            pltpu.VMEM((n, block, HEAD_SIZE), F32),
            pltpu.VMEM((n, block, HEAD_SIZE), F32),
            pltpu.VMEM((rows, width_k), BF16),
            pltpu.VMEM((rows, width_k), BF16),
            pltpu.VMEM((kv_heads, 2, rows, HEAD_SIZE), BF16),
            pltpu.VMEM((kv_heads, 2, rows, HEAD_SIZE), BF16),
            pltpu.VMEM((n, block, width_q), BF16),
            pltpu.VMEM((n, block, width_q), BF16),
            pltpu.VMEM((rows, n * block), BF16),
            pltpu.VMEM((HEAD_SIZE, rows), F32),
            pltpu.VMEM((rows, rows), F32),
            pltpu.VMEM((rows, rows), F32),
            pltpu.VMEM((rows, lanes), F32),
            pltpu.VMEM((HEAD_SIZE, lanes), F32),
            pltpu.VMEM((width_q, rows), F32),
            pltpu.VMEM((rows, width_q), F32),
            pltpu.VMEM((rows, width_k), F32),
            pltpu.VMEM((rows, width_k), F32),
            dma((n,)),
            dma((n,)),
            dma((n,)),
            dma((n,)),
            dma((2,)),
            dma((2,)),
            dma((kv_heads,)),
            dma((kv_heads,)),
            dma((n,)),
            dma((n,)),
            dma((4,)),
        ],
        compiler_params=pltpu.CompilerParams(
            collective_id=0, has_side_effects=True, vmem_limit_bytes=56 * 1024 * 1024
        ),
    )(lengths, plan, query, output_gradient, key, value, lse.T, delta.T)


def solution(mesh):
    rows = P(("grp", "cp"), None)
    return jax.shard_map(
        on_device,
        mesh=mesh,
        in_specs=(rows,) * 6 + (P(), P(("grp", "cp"))),
        out_specs=(rows,) * 3,
        check_vma=False,
    )
```

```python
import functools
import math

import jax
import jax.numpy as jnp
from jax import lax
from jax.experimental import pallas as pl
from jax.experimental.pallas import tpu as pltpu
from jax.sharding import PartitionSpec as P

HEAD_SIZE = 128
FACTOR = HEAD_SIZE**-0.5
LOG2E = math.log2(math.e)
F32 = jnp.float32
BF16 = jnp.bfloat16
MESH = pl.DeviceIdType.MESH


def dot_nt(a, b):
    return lax.dot_general(a, b, (((1,), (1,)), ((), ())), preferred_element_type=F32)


def dot_nn(a, b):
    return jnp.dot(a, b, preferred_element_type=F32)


def group_grads(queries, grads, lse_rows, delta_rows, keys, values, bias):
    keys_t = keys.T
    probs_low, dscores_low, grad_query = [], [], []
    for q, do, lse, delta in zip(queries, grads, lse_rows, delta_rows):
        scores = dot_nt(keys, q)
        probs = jnp.exp2(scores * (FACTOR * LOG2E) + (bias - lse))
        dscores = probs * (dot_nt(values, do) - delta)
        probs_low.append(probs.astype(BF16))
        dscores_low.append(dscores.astype(BF16))
        grad_query.append(dot_nn(keys_t, dscores_low[-1]))
    dv = dot_nn(jnp.concatenate(probs_low, axis=1), jnp.concatenate(grads, axis=0))
    dk = dot_nn(jnp.concatenate(dscores_low, axis=1), jnp.concatenate(queries, axis=0))
    return grad_query, dk, dv


def kernel(
    n,
    groups,
    lengths,
    plan,
    q_hbm,
    do_hbm,
    k_hbm,
    v_hbm,
    lse_ref,
    delta_ref,
    dq_hbm,
    dq_in_hbm,
    dk_hbm,
    dv_hbm,
    q_ref,
    do_ref,
    k_ref,
    v_ref,
    slot_out,
    slot_in,
    stat_out,
    stat_in,
    k_prev,
    v_prev,
    back_out,
    back_in,
    dq_out,
    dq_in,
    stats_t,
    bias_own,
    bias_prev,
    bias_in,
    routed_t,
    dq_t,
    dq_acc,
    dk_acc,
    dv_acc,
    dk_ref,
    dv_ref,
    slot_send,
    slot_recv,
    stat_send,
    stat_recv,
    kv_send,
    kv_recv,
    back_send,
    back_recv,
    dqs_send,
    dqs_recv,
    load_sem,
    store_sem,
):
    grp = lax.axis_index("grp")
    me = lax.axis_index("cp")
    shard = grp * n + me
    last = groups * n - 1
    rows, width_q = q_ref.shape
    width_k = k_ref.shape[1]
    heads = width_q // HEAD_SIZE
    kv_heads = width_k // HEAD_SIZE
    per = heads // kv_heads
    blocks = plan.shape[0]
    block = rows // blocks
    ndocs = lengths.shape[0]
    base = shard * rows
    right = (jnp.where(me == n - 1, jnp.minimum(grp + 1, groups - 1), grp), lax.rem(me + 1, n))
    left = (jnp.where(me == 0, jnp.maximum(grp - 1, 0), grp), lax.rem(me + n - 1, n))
    cross_right = (me == n - 1) & (grp < groups - 1)
    cross_left = (me == 0) & (grp > 0)
    sends = jnp.maximum(me - 1, 0)

    barrier = pltpu.get_barrier_semaphore()
    loads = [
        pltpu.make_async_copy(source, target, load_sem.at[i])
        for i, (source, target) in enumerate(
            ((q_hbm, q_ref), (do_hbm, do_ref), (k_hbm, k_ref), (v_hbm, v_ref))
        )
    ]
    for load in loads:
        load.start()

    def greet(step, carry):
        peer = lax.rem(me + step, n)
        pl.semaphore_signal(barrier, inc=1, device_id=(grp, peer), device_id_type=MESH)
        return carry

    lax.fori_loop(1, n, greet, 0)

    @pl.when(cross_right)
    def _():
        pl.semaphore_signal(barrier, inc=1, device_id=right, device_id_type=MESH)

    @pl.when(cross_left)
    def _():
        pl.semaphore_signal(barrier, inc=1, device_id=left, device_id_type=MESH)

    pos = base + lax.broadcasted_iota(jnp.int32, (8, rows), 1)
    start = jnp.zeros((8, rows), jnp.int32)
    end = jnp.int32(0)
    for d in range(ndocs):
        end = end + lengths[d]
        start = jnp.where(pos >= end, end, start)
    lse_rows = lse_ref[...].astype(F32) * LOG2E
    delta_rows = delta_ref[...].astype(F32)
    pad = HEAD_SIZE - 2 * heads - 16
    packed = jnp.concatenate(
        [
            lse_rows,
            delta_rows,
            start.astype(F32),
            jnp.ones((8, rows), F32),
            jnp.zeros((pad, rows), F32),
        ],
        axis=0,
    )
    stats_t[...] = packed

    count = n * block
    owner = jnp.full((8, rows), -1, jnp.int32)
    token = lax.broadcasted_iota(jnp.int32, (8, rows), 1)
    for b in range(blocks):
        owner = jnp.where((token >= b * block) & (token < (b + 1) * block), plan[b], owner)
    within = lax.rem(token, block)
    slot_row = lax.broadcasted_iota(jnp.int32, (count, rows), 0)
    wanted = owner[:1] * block + within[:1]
    pick = jnp.where((slot_row == wanted) & (owner[:1] >= 0), 1.0, 0.0)
    pick_low = pick.astype(BF16)
    loads[0].wait()
    slot_out[:, :, :width_q] = dot_nn(pick_low, q_ref[...]).astype(BF16).reshape(n, block, width_q)
    loads[1].wait()
    slot_out[:, :, width_q:] = dot_nn(pick_low, do_ref[...]).astype(BF16).reshape(n, block, width_q)
    stat_out[...] = jnp.dot(
        pick, packed.T, preferred_element_type=F32, precision=lax.Precision.HIGHEST
    ).reshape(n, block, HEAD_SIZE)

    def blank_in(p, carry):
        slot_in[p] = jnp.zeros(slot_in.shape[1:], BF16)
        stat_in[p] = jnp.zeros(stat_in.shape[1:], F32)
        return carry

    lax.fori_loop(0, jnp.minimum(me + 2, n), blank_in, 0)

    def blank_dq(p, carry):
        dq_in[p] = jnp.zeros(dq_in.shape[1:], BF16)
        return carry

    lax.fori_loop(sends, n, blank_dq, 0)

    @pl.when(shard == 0)
    def _():
        k_prev[...] = jnp.zeros_like(k_prev)
        v_prev[...] = jnp.zeros_like(v_prev)

    @pl.when(shard == last)
    def _():
        back_in[...] = jnp.zeros_like(back_in)

    pl.semaphore_wait(barrier, n - 1 + cross_right.astype(jnp.int32) + cross_left.astype(jnp.int32))

    def kv_copies():
        return (
            pltpu.make_async_remote_copy(
                k_hbm, k_prev, kv_send.at[0], kv_recv.at[0], device_id=right, device_id_type=MESH
            ),
            pltpu.make_async_remote_copy(
                v_hbm, v_prev, kv_send.at[1], kv_recv.at[1], device_id=right, device_id_type=MESH
            ),
        )

    def slot_copies(p, src):
        return (
            pltpu.make_async_remote_copy(
                slot_out.at[p],
                slot_in.at[src],
                slot_send.at[p],
                slot_recv.at[src],
                device_id=(grp, p),
                device_id_type=MESH,
            ),
            pltpu.make_async_remote_copy(
                stat_out.at[p],
                stat_in.at[src],
                stat_send.at[p],
                stat_recv.at[src],
                device_id=(grp, p),
                device_id_type=MESH,
            ),
        )

    def dq_copy(m, src):
        return pltpu.make_async_remote_copy(
            dq_out.at[m],
            dq_in.at[src],
            dqs_send.at[m],
            dqs_recv.at[src],
            device_id=(grp, m),
            device_id_type=MESH,
        )

    def back_copy(g):
        return pltpu.make_async_remote_copy(
            back_out.at[g],
            back_in.at[g],
            back_send.at[g],
            back_recv.at[g],
            device_id=left,
            device_id_type=MESH,
        )

    @pl.when(shard < last)
    def _():
        for copy in kv_copies():
            copy.start()

    def send(p, carry):
        for copy in slot_copies(p, me):
            copy.start()
        return carry

    lax.fori_loop(0, sends, send, 0)

    key_at = lax.broadcasted_iota(jnp.int32, (rows, rows), 0)
    query_at = lax.broadcasted_iota(jnp.int32, (rows, rows), 1)
    begin = start[:1] - base
    bias_own[...] = jnp.where((key_at <= query_at) & (key_at >= begin), 0.0, -jnp.inf)
    bias_prev[...] = jnp.where(key_at - rows >= begin, 0.0, -jnp.inf)

    def columns(h):
        return pl.ds(pl.multiple_of(h * HEAD_SIZE, HEAD_SIZE), HEAD_SIZE)

    def local_inputs(g):
        hs = [g * per + u for u in range(per)]
        return (
            [q_ref[:, columns(h)] for h in hs],
            [do_ref[:, columns(h)] for h in hs],
            [stats_t[pl.ds(h, 1), :] for h in hs],
            [stats_t[pl.ds(heads + h, 1), :] for h in hs],
        )

    def own(g, carry):
        cols = columns(g)
        grad_query, dk, dv = group_grads(
            *local_inputs(g), k_ref[:, cols], v_ref[:, cols], bias_own[...]
        )
        for u in range(per):
            dq_t[columns(g * per + u), :] = grad_query[u]
        dk_acc[:, cols] = dk
        dv_acc[:, cols] = dv
        return carry

    loads[2].wait()
    loads[3].wait()
    lax.fori_loop(0, kv_heads, own, 0)

    @pl.when(shard > 0)
    def _():
        for copy in kv_copies():
            copy.wait_recv()

    def prev(g, carry):
        cols = columns(g)
        grad_query, dk, dv = group_grads(
            *local_inputs(g), k_prev[:, cols], v_prev[:, cols], bias_prev[...]
        )
        for u in range(per):
            where = columns(g * per + u)
            dq_acc[:, where] = ((dq_t[where, :] + grad_query[u]) * FACTOR).T.astype(BF16)
        back_out[g, 0] = (dk * FACTOR).astype(BF16)
        back_out[g, 1] = dv.astype(BF16)

        @pl.when(shard > 0)
        def _():
            back_copy(g).start()

        return carry

    lax.fori_loop(0, kv_heads, prev, 0)
    stores = [
        pltpu.make_async_copy(source, target, store_sem.at[i])
        for i, (source, target) in enumerate(
            ((dq_acc, dq_hbm), (dk_ref, dk_hbm), (dv_ref, dv_hbm), (dq_in, dq_in_hbm))
        )
    ]
    stores[0].start()

    half = 2 * block
    lanes = per * half
    lane_head = lax.broadcasted_iota(jnp.int32, (1, lanes), 1) // half
    key_pos = base + lax.broadcasted_iota(jnp.int32, (rows, lanes), 0)

    def batch(j, carry):
        m = 2 * j

        @pl.when(m >= me + 2)
        def _():
            for copy in slot_copies(m, m):
                copy.wait_recv()

        for copy in slot_copies(m + 1, m + 1):
            copy.wait_recv()
        pair = pl.ds(m, 2)
        stat = stat_in[pair].reshape(half, HEAD_SIZE)
        routed_t[...] = jnp.concatenate([stat] * per, axis=0).T
        first = routed_t[pl.ds(2 * heads, 1), :]
        live = routed_t[pl.ds(2 * heads + 8, 1), :] > 0.5
        bias_in[...] = jnp.where((key_pos.astype(F32) >= first) & live, 0.0, -jnp.inf)

        def row_of(first_row):
            out = routed_t[pl.ds(first_row, 1), :]
            for u in range(1, per):
                out = jnp.where(lane_head == u, routed_t[pl.ds(first_row + u, 1), :], out)
            return out

        def routed(g, carry):
            cols = columns(g)
            hs = [g * per + u for u in range(per)]

            def stack(offset):
                return jnp.concatenate(
                    [
                        slot_in[pair, :, columns(offset + h)].reshape(half, HEAD_SIZE)
                        for h in hs
                    ],
                    axis=0,
                )

            grad_query, dk, dv = group_grads(
                [stack(0)],
                [stack(heads)],
                [row_of(g * per)],
                [row_of(heads + g * per)],
                k_ref[:, cols],
                v_ref[:, cols],
                bias_in[...],
            )
            back = (grad_query[0] * FACTOR).T.astype(BF16)
            for u in range(per):
                dq_out[pair, :, columns(hs[u])] = back[u * half : (u + 1) * half].reshape(
                    2, block, HEAD_SIZE
                )
            dk_acc[:, cols] += dk
            dv_acc[:, cols] += dv
            return carry

        lax.fori_loop(0, kv_heads, routed, 0)

        @pl.when(m >= me + 2)
        def _():
            dq_copy(m, me).start()

        dq_copy(m + 1, me).start()
        return carry

    lax.fori_loop((me + 2) // 2, n // 2, batch, 0)

    for g in range(kv_heads):

        @pl.when(shard < last)
        def _(g=g):
            back_copy(g).wait_recv()

        cols = pl.ds(g * HEAD_SIZE, HEAD_SIZE)
        dk_ref[:, cols] = (dk_acc[:, cols] * FACTOR + back_in[g, 0].astype(F32)).astype(BF16)
        dv_ref[:, cols] = (dv_acc[:, cols] + back_in[g, 1].astype(F32)).astype(BF16)

    stores[1].start()
    stores[2].start()

    def take(p, carry):
        dq_copy(p, p).wait_recv()
        return carry

    lax.fori_loop(0, sends, take, 0)
    stores[3].start()

    @pl.when(shard < last)
    def _():
        for copy in kv_copies():
            copy.wait_send()

    @pl.when(shard > 0)
    def _():
        for g in range(kv_heads):
            back_copy(g).wait_send()

    def sent(p, carry):
        for copy in slot_copies(p, me):
            copy.wait_send()
        return carry

    lax.fori_loop(0, sends, sent, 0)

    def sent_back(m, carry):
        dq_copy(m, me).wait_send()
        return carry

    lax.fori_loop(me + 2, n, sent_back, 0)
    for store in stores:
        store.wait()


def finish(plan, dq_near, dq_far, dk, dv, dq_ref, dk_ref, dv_ref):
    block = dq_far.shape[1]
    blocks = dq_near.shape[0] // block
    first = pl.program_id(0) * blocks
    for b in range(blocks):
        owner = plan[first + b]
        at = pl.ds(b * block, block)
        near = dq_near[at, :].astype(F32)
        far = dq_far[jnp.maximum(owner, 0)].astype(F32)
        dq_ref[at, :] = jnp.where(owner >= 0, near + far, near).astype(BF16)
    dk_ref[...] = dk[...]
    dv_ref[...] = dv[...]


def on_device(query, key, value, output_gradient, lse, delta, lengths, plan):
    n = lax.axis_size("cp")
    groups = lax.axis_size("grp")
    rows, width_q = query.shape
    width_k = key.shape[1]
    kv_heads = width_k // HEAD_SIZE
    block = rows // plan.shape[0]
    lanes = 2 * block * (width_q // width_k)
    vmem = pl.BlockSpec(memory_space=pltpu.VMEM)
    smem = pl.BlockSpec(memory_space=pltpu.SMEM)
    dma = pltpu.SemaphoreType.DMA
    anywhere = pl.BlockSpec(memory_space=pl.ANY)
    parts = pl.pallas_call(
        functools.partial(kernel, n, groups),
        out_shape=(
            jax.ShapeDtypeStruct((rows, width_q), BF16),
            jax.ShapeDtypeStruct((n, block, width_q), BF16),
            jax.ShapeDtypeStruct((rows, width_k), BF16),
            jax.ShapeDtypeStruct((rows, width_k), BF16),
        ),
        in_specs=[smem, smem] + [anywhere] * 4 + [vmem] * 2,
        out_specs=[anywhere] * 4,
        scratch_shapes=[
            pltpu.VMEM((rows, width_q), BF16),
            pltpu.VMEM((rows, width_q), BF16),
            pltpu.VMEM((rows, width_k), BF16),
            pltpu.VMEM((rows, width_k), BF16),
            pltpu.VMEM((n, block, 2 * width_q), BF16),
            pltpu.VMEM((n, block, 2 * width_q), BF16),
            pltpu.VMEM((n, block, HEAD_SIZE), F32),
            pltpu.VMEM((n, block, HEAD_SIZE), F32),
            pltpu.VMEM((rows, width_k), BF16),
            pltpu.VMEM((rows, width_k), BF16),
            pltpu.VMEM((kv_heads, 2, rows, HEAD_SIZE), BF16),
            pltpu.VMEM((kv_heads, 2, rows, HEAD_SIZE), BF16),
            pltpu.VMEM((n, block, width_q), BF16),
            pltpu.VMEM((n, block, width_q), BF16),
            pltpu.VMEM((HEAD_SIZE, rows), F32),
            pltpu.VMEM((rows, rows), F32),
            pltpu.VMEM((rows, rows), F32),
            pltpu.VMEM((rows, lanes), F32),
            pltpu.VMEM((HEAD_SIZE, lanes), F32),
            pltpu.VMEM((width_q, rows), F32),
            pltpu.VMEM((rows, width_q), BF16),
            pltpu.VMEM((rows, width_k), F32),
            pltpu.VMEM((rows, width_k), F32),
            pltpu.VMEM((rows, width_k), BF16),
            pltpu.VMEM((rows, width_k), BF16),
            dma((n,)),
            dma((n,)),
            dma((n,)),
            dma((n,)),
            dma((2,)),
            dma((2,)),
            dma((kv_heads,)),
            dma((kv_heads,)),
            dma((n,)),
            dma((n,)),
            dma((4,)),
            dma((4,)),
        ],
        compiler_params=pltpu.CompilerParams(
            collective_id=0, has_side_effects=True, vmem_limit_bytes=56 * 1024 * 1024
        ),
    )(lengths, plan, query, output_gradient, key, value, lse.T, delta.T)
    steps = 4
    wide = pl.BlockSpec((rows // steps, width_q), lambda i, plan: (i, 0))
    narrow = pl.BlockSpec((rows // steps, width_k), lambda i, plan: (i, 0))
    whole = pl.BlockSpec((n, block, width_q), lambda i, plan: (0, 0, 0))
    return pl.pallas_call(
        finish,
        out_shape=(
            jax.ShapeDtypeStruct((rows, width_q), BF16),
            jax.ShapeDtypeStruct((rows, width_k), BF16),
            jax.ShapeDtypeStruct((rows, width_k), BF16),
        ),
        grid_spec=pltpu.PrefetchScalarGridSpec(
            num_scalar_prefetch=1,
            grid=(steps,),
            in_specs=[wide, whole, narrow, narrow],
            out_specs=[wide, narrow, narrow],
        ),
    )(plan, *parts)


def solution(mesh):
    rows = P(("grp", "cp"), None)
    return jax.shard_map(
        on_device,
        mesh=mesh,
        in_specs=(rows,) * 6 + (P(), P(("grp", "cp"))),
        out_specs=(rows,) * 3,
        check_vma=False,
    )
```

```python
import functools
import math

import jax
import jax.numpy as jnp
from jax import lax
from jax.experimental import pallas as pl
from jax.experimental.pallas import tpu as pltpu
from jax.sharding import PartitionSpec as P

HEAD_SIZE = 128
FACTOR = HEAD_SIZE**-0.5
LOG2E = math.log2(math.e)
F32 = jnp.float32
BF16 = jnp.bfloat16
MESH = pl.DeviceIdType.MESH


def dot_nt(a, b):
    return lax.dot_general(a, b, (((1,), (1,)), ((), ())), preferred_element_type=F32)


def dot_nn(a, b):
    return jnp.dot(a, b, preferred_element_type=F32)


def group_grads(queries, grads, lse_rows, delta_rows, keys, values, bias):
    keys_t = keys.T
    probs_low, dscores_low, grad_query = [], [], []
    for q, do, lse, delta in zip(queries, grads, lse_rows, delta_rows):
        scores = dot_nt(keys, q)
        probs = jnp.exp2(scores * (FACTOR * LOG2E) + (bias - lse))
        dscores = probs * (dot_nt(values, do) - delta)
        probs_low.append(probs.astype(BF16))
        dscores_low.append(dscores.astype(BF16))
        grad_query.append(dot_nn(keys_t, dscores_low[-1]))
    dv = dot_nn(jnp.concatenate(probs_low, axis=1), jnp.concatenate(grads, axis=0))
    dk = dot_nn(jnp.concatenate(dscores_low, axis=1), jnp.concatenate(queries, axis=0))
    return grad_query, dk, dv


def kernel(
    n,
    groups,
    lengths,
    plan,
    q_hbm,
    do_hbm,
    k_hbm,
    v_hbm,
    lse_ref,
    delta_ref,
    dq_hbm,
    dq_in_hbm,
    dk_hbm,
    dv_hbm,
    q_ref,
    do_ref,
    k_ref,
    v_ref,
    slot_out,
    slot_in,
    stat_out,
    stat_in,
    k_prev,
    v_prev,
    back_out,
    back_in,
    dq_out,
    dq_in,
    stats_t,
    bias_own,
    bias_prev,
    bias_in,
    routed_t,
    dq_t,
    dq_acc,
    dk_acc,
    dv_acc,
    dk_ref,
    dv_ref,
    slot_send,
    slot_recv,
    stat_send,
    stat_recv,
    kv_send,
    kv_recv,
    back_send,
    back_recv,
    dqs_send,
    dqs_recv,
    load_sem,
    store_sem,
):
    grp = lax.axis_index("grp")
    me = lax.axis_index("cp")
    shard = grp * n + me
    last = groups * n - 1
    rows, width_q = q_ref.shape
    width_k = k_ref.shape[1]
    heads = width_q // HEAD_SIZE
    kv_heads = width_k // HEAD_SIZE
    per = heads // kv_heads
    blocks = plan.shape[0]
    block = rows // blocks
    ndocs = lengths.shape[0]
    base = shard * rows
    right = (jnp.where(me == n - 1, jnp.minimum(grp + 1, groups - 1), grp), lax.rem(me + 1, n))
    left = (jnp.where(me == 0, jnp.maximum(grp - 1, 0), grp), lax.rem(me + n - 1, n))
    cross_right = (me == n - 1) & (grp < groups - 1)
    cross_left = (me == 0) & (grp > 0)
    sends = jnp.maximum(me - 1, 0)

    barrier = pltpu.get_barrier_semaphore()
    loads = [
        pltpu.make_async_copy(source, target, load_sem.at[i])
        for i, (source, target) in enumerate(
            ((q_hbm, q_ref), (do_hbm, do_ref), (k_hbm, k_ref), (v_hbm, v_ref))
        )
    ]
    for load in loads:
        load.start()

    def greet(step, carry):
        peer = lax.rem(me + step, n)
        pl.semaphore_signal(barrier, inc=1, device_id=(grp, peer), device_id_type=MESH)
        return carry

    lax.fori_loop(1, n, greet, 0)

    @pl.when(cross_right)
    def _():
        pl.semaphore_signal(barrier, inc=1, device_id=right, device_id_type=MESH)

    @pl.when(cross_left)
    def _():
        pl.semaphore_signal(barrier, inc=1, device_id=left, device_id_type=MESH)

    pos = base + lax.broadcasted_iota(jnp.int32, (8, rows), 1)
    start = jnp.zeros((8, rows), jnp.int32)
    end = jnp.int32(0)
    for d in range(ndocs):
        end = end + lengths[d]
        start = jnp.where(pos >= end, end, start)
    lse_rows = lse_ref[...].astype(F32) * LOG2E
    delta_rows = delta_ref[...].astype(F32)
    pad = HEAD_SIZE - 2 * heads - 16
    packed = jnp.concatenate(
        [
            lse_rows,
            delta_rows,
            start.astype(F32),
            jnp.ones((8, rows), F32),
            jnp.zeros((pad, rows), F32),
        ],
        axis=0,
    )
    stats_t[...] = packed

    count = n * block
    owner = jnp.full((8, rows), -1, jnp.int32)
    token = lax.broadcasted_iota(jnp.int32, (8, rows), 1)
    for b in range(blocks):
        owner = jnp.where((token >= b * block) & (token < (b + 1) * block), plan[b], owner)
    within = lax.rem(token, block)
    slot_row = lax.broadcasted_iota(jnp.int32, (count, rows), 0)
    wanted = owner[:1] * block + within[:1]
    pick = jnp.where((slot_row == wanted) & (owner[:1] >= 0), 1.0, 0.0)
    pick_low = pick.astype(BF16)
    loads[0].wait()
    slot_out[:, :, :width_q] = dot_nn(pick_low, q_ref[...]).astype(BF16).reshape(n, block, width_q)
    loads[1].wait()
    slot_out[:, :, width_q:] = dot_nn(pick_low, do_ref[...]).astype(BF16).reshape(n, block, width_q)
    stat_out[...] = jnp.dot(
        pick, packed.T, preferred_element_type=F32, precision=lax.Precision.HIGHEST
    ).reshape(n, block, HEAD_SIZE)

    def blank_in(p, carry):
        slot_in[p] = jnp.zeros(slot_in.shape[1:], BF16)
        stat_in[p] = jnp.zeros(stat_in.shape[1:], F32)
        return carry

    lax.fori_loop(0, jnp.minimum(me + 2, n), blank_in, 0)

    def blank_dq(p, carry):
        dq_in[p] = jnp.zeros(dq_in.shape[1:], BF16)
        return carry

    lax.fori_loop(sends, n, blank_dq, 0)

    @pl.when(shard == 0)
    def _():
        k_prev[...] = jnp.zeros_like(k_prev)
        v_prev[...] = jnp.zeros_like(v_prev)

    @pl.when(shard == last)
    def _():
        back_in[...] = jnp.zeros_like(back_in)

    pl.semaphore_wait(barrier, n - 1 + cross_right.astype(jnp.int32) + cross_left.astype(jnp.int32))

    def kv_copies():
        return (
            pltpu.make_async_remote_copy(
                k_hbm, k_prev, kv_send.at[0], kv_recv.at[0], device_id=right, device_id_type=MESH
            ),
            pltpu.make_async_remote_copy(
                v_hbm, v_prev, kv_send.at[1], kv_recv.at[1], device_id=right, device_id_type=MESH
            ),
        )

    def slot_copies(p, src):
        return (
            pltpu.make_async_remote_copy(
                slot_out.at[p],
                slot_in.at[src],
                slot_send.at[p],
                slot_recv.at[src],
                device_id=(grp, p),
                device_id_type=MESH,
            ),
            pltpu.make_async_remote_copy(
                stat_out.at[p],
                stat_in.at[src],
                stat_send.at[p],
                stat_recv.at[src],
                device_id=(grp, p),
                device_id_type=MESH,
            ),
        )

    def dq_copy(m, src):
        return pltpu.make_async_remote_copy(
            dq_out.at[m],
            dq_in.at[src],
            dqs_send.at[m],
            dqs_recv.at[src],
            device_id=(grp, m),
            device_id_type=MESH,
        )

    def back_copy(g):
        return pltpu.make_async_remote_copy(
            back_out.at[g],
            back_in.at[g],
            back_send.at[g],
            back_recv.at[g],
            device_id=left,
            device_id_type=MESH,
        )

    @pl.when(shard < last)
    def _():
        for copy in kv_copies():
            copy.start()

    def send(p, carry):
        for copy in slot_copies(p, me):
            copy.start()
        return carry

    lax.fori_loop(0, sends, send, 0)

    key_at = lax.broadcasted_iota(jnp.int32, (rows, rows), 0)
    query_at = lax.broadcasted_iota(jnp.int32, (rows, rows), 1)
    begin = start[:1] - base
    bias_own[...] = jnp.where((key_at <= query_at) & (key_at >= begin), 0.0, -jnp.inf)
    bias_prev[...] = jnp.where(key_at - rows >= begin, 0.0, -jnp.inf)

    def columns(h):
        return pl.ds(pl.multiple_of(h * HEAD_SIZE, HEAD_SIZE), HEAD_SIZE)

    def local_inputs(g):
        hs = [g * per + u for u in range(per)]
        return (
            [q_ref[:, columns(h)] for h in hs],
            [do_ref[:, columns(h)] for h in hs],
            [stats_t[pl.ds(h, 1), :] for h in hs],
            [stats_t[pl.ds(heads + h, 1), :] for h in hs],
        )

    def own(g, carry):
        cols = columns(g)
        grad_query, dk, dv = group_grads(
            *local_inputs(g), k_ref[:, cols], v_ref[:, cols], bias_own[...]
        )
        for u in range(per):
            dq_t[columns(g * per + u), :] = grad_query[u]
        dk_acc[:, cols] = dk
        dv_acc[:, cols] = dv
        return carry

    loads[2].wait()
    loads[3].wait()
    lax.fori_loop(0, kv_heads, own, 0)

    @pl.when(shard > 0)
    def _():
        for copy in kv_copies():
            copy.wait_recv()

    def prev(g, carry):
        cols = columns(g)
        grad_query, dk, dv = group_grads(
            *local_inputs(g), k_prev[:, cols], v_prev[:, cols], bias_prev[...]
        )
        for u in range(per):
            where = columns(g * per + u)
            dq_acc[:, where] = ((dq_t[where, :] + grad_query[u]) * FACTOR).T.astype(BF16)
        back_out[g, 0] = (dk * FACTOR).astype(BF16)
        back_out[g, 1] = dv.astype(BF16)

        @pl.when(shard > 0)
        def _():
            back_copy(g).start()

        return carry

    lax.fori_loop(0, kv_heads, prev, 0)
    stores = [
        pltpu.make_async_copy(source, target, store_sem.at[i])
        for i, (source, target) in enumerate(
            ((dq_acc, dq_hbm), (dk_ref, dk_hbm), (dv_ref, dv_hbm), (dq_in, dq_in_hbm))
        )
    ]
    stores[0].start()

    half = 2 * block
    lanes = per * half
    lane_head = lax.broadcasted_iota(jnp.int32, (1, lanes), 1) // half
    key_pos = base + lax.broadcasted_iota(jnp.int32, (rows, lanes), 0)

    def batch(j, carry):
        m = n - 2 - 2 * j

        @pl.when(m >= me + 2)
        def _():
            for copy in slot_copies(m, m):
                copy.wait_recv()

        for copy in slot_copies(m + 1, m + 1):
            copy.wait_recv()
        pair = pl.ds(m, 2)
        stat = stat_in[pair].reshape(half, HEAD_SIZE)
        routed_t[...] = jnp.concatenate([stat] * per, axis=0).T
        first = routed_t[pl.ds(2 * heads, 1), :]
        live = routed_t[pl.ds(2 * heads + 8, 1), :] > 0.5
        bias_in[...] = jnp.where((key_pos.astype(F32) >= first) & live, 0.0, -jnp.inf)

        def row_of(first_row):
            out = routed_t[pl.ds(first_row, 1), :]
            for u in range(1, per):
                out = jnp.where(lane_head == u, routed_t[pl.ds(first_row + u, 1), :], out)
            return out

        def routed(g, carry):
            cols = columns(g)
            hs = [g * per + u for u in range(per)]

            def stack(offset):
                return jnp.concatenate(
                    [
                        slot_in[pair, :, columns(offset + h)].reshape(half, HEAD_SIZE)
                        for h in hs
                    ],
                    axis=0,
                )

            grad_query, dk, dv = group_grads(
                [stack(0)],
                [stack(heads)],
                [row_of(g * per)],
                [row_of(heads + g * per)],
                k_ref[:, cols],
                v_ref[:, cols],
                bias_in[...],
            )
            back = (grad_query[0] * FACTOR).T.astype(BF16)
            for u in range(per):
                dq_out[pair, :, columns(hs[u])] = back[u * half : (u + 1) * half].reshape(
                    2, block, HEAD_SIZE
                )
            dk_acc[:, cols] += dk
            dv_acc[:, cols] += dv
            return carry

        lax.fori_loop(0, kv_heads, routed, 0)

        @pl.when(m >= me + 2)
        def _():
            dq_copy(m, me).start()

        dq_copy(m + 1, me).start()
        return carry

    lax.fori_loop(0, n // 2 - (me + 2) // 2, batch, 0)

    for g in range(kv_heads):

        @pl.when(shard < last)
        def _(g=g):
            back_copy(g).wait_recv()

        cols = pl.ds(g * HEAD_SIZE, HEAD_SIZE)
        dk_ref[:, cols] = (dk_acc[:, cols] * FACTOR + back_in[g, 0].astype(F32)).astype(BF16)
        dv_ref[:, cols] = (dv_acc[:, cols] + back_in[g, 1].astype(F32)).astype(BF16)

    stores[1].start()
    stores[2].start()

    def take(p, carry):
        dq_copy(p, p).wait_recv()
        return carry

    lax.fori_loop(0, sends, take, 0)
    stores[3].start()

    @pl.when(shard < last)
    def _():
        for copy in kv_copies():
            copy.wait_send()

    @pl.when(shard > 0)
    def _():
        for g in range(kv_heads):
            back_copy(g).wait_send()

    def sent(p, carry):
        for copy in slot_copies(p, me):
            copy.wait_send()
        return carry

    lax.fori_loop(0, sends, sent, 0)

    def sent_back(m, carry):
        dq_copy(m, me).wait_send()
        return carry

    lax.fori_loop(me + 2, n, sent_back, 0)
    for store in stores:
        store.wait()


def finish(plan, dq_near, dq_far, dk, dv, dq_ref, dk_ref, dv_ref):
    block = dq_far.shape[1]
    blocks = dq_near.shape[0] // block
    first = pl.program_id(0) * blocks
    for b in range(blocks):
        owner = plan[first + b]
        at = pl.ds(b * block, block)
        near = dq_near[at, :].astype(F32)
        far = dq_far[jnp.maximum(owner, 0)].astype(F32)
        dq_ref[at, :] = jnp.where(owner >= 0, near + far, near).astype(BF16)
    dk_ref[...] = dk[...]
    dv_ref[...] = dv[...]


def on_device(query, key, value, output_gradient, lse, delta, lengths, plan):
    n = lax.axis_size("cp")
    groups = lax.axis_size("grp")
    rows, width_q = query.shape
    width_k = key.shape[1]
    kv_heads = width_k // HEAD_SIZE
    block = rows // plan.shape[0]
    lanes = 2 * block * (width_q // width_k)
    vmem = pl.BlockSpec(memory_space=pltpu.VMEM)
    smem = pl.BlockSpec(memory_space=pltpu.SMEM)
    dma = pltpu.SemaphoreType.DMA
    anywhere = pl.BlockSpec(memory_space=pl.ANY)
    parts = pl.pallas_call(
        functools.partial(kernel, n, groups),
        out_shape=(
            jax.ShapeDtypeStruct((rows, width_q), BF16),
            jax.ShapeDtypeStruct((n, block, width_q), BF16),
            jax.ShapeDtypeStruct((rows, width_k), BF16),
            jax.ShapeDtypeStruct((rows, width_k), BF16),
        ),
        in_specs=[smem, smem] + [anywhere] * 4 + [vmem] * 2,
        out_specs=[anywhere] * 4,
        scratch_shapes=[
            pltpu.VMEM((rows, width_q), BF16),
            pltpu.VMEM((rows, width_q), BF16),
            pltpu.VMEM((rows, width_k), BF16),
            pltpu.VMEM((rows, width_k), BF16),
            pltpu.VMEM((n, block, 2 * width_q), BF16),
            pltpu.VMEM((n, block, 2 * width_q), BF16),
            pltpu.VMEM((n, block, HEAD_SIZE), F32),
            pltpu.VMEM((n, block, HEAD_SIZE), F32),
            pltpu.VMEM((rows, width_k), BF16),
            pltpu.VMEM((rows, width_k), BF16),
            pltpu.VMEM((kv_heads, 2, rows, HEAD_SIZE), BF16),
            pltpu.VMEM((kv_heads, 2, rows, HEAD_SIZE), BF16),
            pltpu.VMEM((n, block, width_q), BF16),
            pltpu.VMEM((n, block, width_q), BF16),
            pltpu.VMEM((HEAD_SIZE, rows), F32),
            pltpu.VMEM((rows, rows), F32),
            pltpu.VMEM((rows, rows), F32),
            pltpu.VMEM((rows, lanes), F32),
            pltpu.VMEM((HEAD_SIZE, lanes), F32),
            pltpu.VMEM((width_q, rows), F32),
            pltpu.VMEM((rows, width_q), BF16),
            pltpu.VMEM((rows, width_k), F32),
            pltpu.VMEM((rows, width_k), F32),
            pltpu.VMEM((rows, width_k), BF16),
            pltpu.VMEM((rows, width_k), BF16),
            dma((n,)),
            dma((n,)),
            dma((n,)),
            dma((n,)),
            dma((2,)),
            dma((2,)),
            dma((kv_heads,)),
            dma((kv_heads,)),
            dma((n,)),
            dma((n,)),
            dma((4,)),
            dma((4,)),
        ],
        compiler_params=pltpu.CompilerParams(
            collective_id=0, has_side_effects=True, vmem_limit_bytes=56 * 1024 * 1024
        ),
    )(lengths, plan, query, output_gradient, key, value, lse.T, delta.T)
    steps = 2
    wide = pl.BlockSpec((rows // steps, width_q), lambda i, plan: (i, 0))
    narrow = pl.BlockSpec((rows // steps, width_k), lambda i, plan: (i, 0))
    whole = pl.BlockSpec((n, block, width_q), lambda i, plan: (0, 0, 0))
    return pl.pallas_call(
        finish,
        out_shape=(
            jax.ShapeDtypeStruct((rows, width_q), BF16),
            jax.ShapeDtypeStruct((rows, width_k), BF16),
            jax.ShapeDtypeStruct((rows, width_k), BF16),
        ),
        grid_spec=pltpu.PrefetchScalarGridSpec(
            num_scalar_prefetch=1,
            grid=(steps,),
            in_specs=[wide, whole, narrow, narrow],
            out_specs=[wide, narrow, narrow],
        ),
    )(plan, *parts)


def solution(mesh):
    rows = P(("grp", "cp"), None)
    return jax.shard_map(
        on_device,
        mesh=mesh,
        in_specs=(rows,) * 6 + (P(), P(("grp", "cp"))),
        out_specs=(rows,) * 3,
        check_vma=False,
    )
```
